32 devices in a mesh: section: 4 (over y, core), hid: 8 (over z, x).
Axes of the slice: x: 2, y: 2, z: 4, core: 2. Of those that a mesh axis runs over, the one named last changes fastest.
Arguments:
- streams: float32 [4, 2, 512, 1024], P('section', None, 'hid'), may hold values from -6 to 6
- cotangents: float32 [4, 2, 512, 1024], P('section', None, 'hid'), may hold values from -0.6 to 0.6
- feed_streams: float32 [2, 2, 512, 1024], P(None, None, 'hid'), may hold values from -6 to 6
- feed_cotangents: float32 [2, 2, 512, 1024], P(None, None, 'hid'), may hold values from -0.6 to 0.6
- w_in: bfloat16 [4, 1024, 16384], P('section', None, 'hid'), may hold values from -0.1875 to 0.1875
- w_out: bfloat16 [4, 16384, 1024], P('section', 'hid'), may hold values from -0.046875 to 0.046875
- gain: float32 [4, 1024], P('section'), may hold values from 0.1 to 1.9
Outputs:
- out_streams: float32 [4, 2, 512, 1024], P('section', None, 'hid')
- out_cotangents: float32 [4, 2, 512, 1024], P('section', None, 'hid')
- grad_in: float32 [4, 1024, 16384], P('section', None, 'hid')
- grad_out: float32 [4, 16384, 1024], P('section', 'hid')
The draws below stay inside these ranges and needn't reach their ends.
All inputs are finite; a program needn't handle non-finite values.
Results may differ from the reference program's by a relative error of at most 0.0071.
Values may be sent and summed in bfloat16 or wider, within the bound.
No kernel may reach another device: no remote copies, remote signals or barrier semaphores. Data moves between devices by JAX's collectives and lax.ppermute only.
A program may use at most 128 MiB of HBM per device.

```python
from functools import partial
import jax
import jax.numpy as jnp
from jax import lax

D = 1024
FF = 16384
ROWS = 512
TICKS = 3
SECTIONS = 4


def block_scale(rng, dims, shards, smallest, top_value):
    def one(axis_at, shards_of):
        draws = jax.random.uniform(jax.random.fold_in(jax.random.fold_in(rng, 6), axis_at), (shards_of,), jnp.float32, smallest / len(shards), top_value / len(shards))
        return jnp.repeat(jnp.exp(draws), dims[axis_at] // shards_of).reshape((-1,) + (1,) * (len(dims) - axis_at - 1))

    loudness = one(*shards[0])
    for cut in shards[1:]:
        loudness = loudness * one(*cut)
    return loudness


def centred(own_key, dims, deviation, limit, cuts=(), dtype=jnp.bfloat16):
    result = deviation * jax.random.normal(own_key, dims, jnp.float32)
    if cuts:
        result = result * block_scale(own_key, dims, cuts, -0.22, 0.18)
    return jnp.clip(result, -limit, limit).astype(dtype)


def setup_inputs(seed: int = 0) -> dict:
    streams_of = jax.random.split(jax.random.key(seed), 8)
    return {
        "streams": centred(streams_of[0], (SECTIONS, 2, ROWS, D), 1.0, 6.0, ((0, 4), (2, 8)), jnp.float32),
        "cotangents": centred(streams_of[1], (SECTIONS, 2, ROWS, D), 0.1, 0.6, ((0, 4), (2, 8)), jnp.float32),
        "feed_streams": centred(streams_of[2], (TICKS - 1, 2, ROWS, D), 1.0, 6.0, ((2, 8),), jnp.float32),
        "feed_cotangents": centred(streams_of[3], (TICKS - 1, 2, ROWS, D), 0.1, 0.6, ((2, 8),), jnp.float32),
        "w_in": centred(streams_of[4], (SECTIONS, D, FF), D ** -0.5, 0.1875, ((0, 4), (2, 8))),
        "w_out": centred(streams_of[5], (SECTIONS, FF, D), FF ** -0.5, 0.046875, ((0, 4), (1, 8))),
        "gain": jnp.clip(1.0 + 0.18 * jax.random.normal(streams_of[6], (SECTIONS, D), jnp.float32), 0.1, 1.9),
    }


def normalize(stream):
    mean_sq = lax.optimization_barrier(jnp.mean(stream * stream, axis=-1, keepdims=True))
    scale_row = lax.rsqrt(mean_sq + 1e-06)
    return (stream * scale_row, scale_row)

def back_step(first, second, grad_first, grad_second, weight_in, weight_out, gain_row):
    normed, scale_row = normalize(first)
    lifted = (normed * gain_row).astype(jnp.bfloat16)
    pre = jnp.dot(lifted, weight_in, preferred_element_type=jnp.float32)
    hidden = jax.nn.gelu(pre, approximate=True).astype(jnp.bfloat16)
    restored = second - jnp.dot(hidden, weight_out, preferred_element_type=jnp.float32)
    cotan = grad_second.astype(jnp.bfloat16)
    back_hidden = jnp.dot(cotan, weight_out.T, preferred_element_type=jnp.float32)
    unused, pull = jax.vjp(partial(jax.nn.gelu, approximate=True), pre)
    back_pre = pull(back_hidden)[0].astype(jnp.bfloat16)
    back_lift = jnp.dot(back_pre, weight_in.T, preferred_element_type=jnp.float32)
    back_norm = back_lift * gain_row
    grad_stream = grad_first + scale_row * (back_norm - normed * lax.optimization_barrier(jnp.mean(back_norm * normed, axis=-1, keepdims=True)))
    grad_win = jnp.dot(lifted.T, back_pre, preferred_element_type=jnp.float32)
    grad_wout = jnp.dot(hidden.T, cotan, preferred_element_type=jnp.float32)
    return (restored, grad_stream, grad_win, grad_wout)

def one_section(items):
    held, held_cot, weight_in, weight_out, gain_row = items
    restored, grad_stream, grad_win, grad_wout = back_step(held[0], held[1], held_cot[0], held_cot[1], weight_in, weight_out, gain_row)
    new_streams = jnp.stack([restored, held[0]])
    new_cot = jnp.stack([held_cot[1], grad_stream])
    return (new_streams, new_cot, grad_win, grad_wout)

def reference(streams, cotangents, feed_streams, feed_cotangents, w_in, w_out, gain):
    total_in = jnp.zeros(w_in.shape, jnp.float32)
    total_out = jnp.zeros(w_out.shape, jnp.float32)
    held, held_cot = (streams, cotangents)
    for tick_num in range(TICKS):
        new_streams, new_cot, grad_win, grad_wout = lax.map(one_section, (held, held_cot, w_in, w_out, gain))
        total_in = total_in + grad_win
        total_out = total_out + grad_wout
        if tick_num < TICKS - 1:
            held = jnp.concatenate([new_streams[1:], feed_streams[tick_num][None]], axis=0)
            held_cot = jnp.concatenate([new_cot[1:], feed_cotangents[tick_num][None]], axis=0)
    return (new_streams, new_cot, total_in, total_out)
```

```python
import math

import jax
import jax.numpy as jnp
from jax import lax
from jax.sharding import PartitionSpec as P


def swap(value, bit):
    count = lax.axis_size("hid")
    return lax.ppermute(value, "hid", [(i, i ^ bit) for i in range(count)])


def down(value):
    count = lax.axis_size("section")
    return lax.ppermute(value, "section", [(i, i - 1) for i in range(1, count)])


def gather(own, bits):
    near = own
    for bit in bits[:-2]:
        near = jnp.concatenate([near, swap(near, bit)], axis=0)
    near_b = swap(near, bits[-2])
    far_a = swap(near, bits[-1])
    far_b = swap(near_b, bits[-1])
    return (
        jnp.concatenate([near, near_b], axis=0),
        jnp.concatenate([far_a, far_b], axis=0),
    )


def reduce(near, far, bits):
    half = far.shape[0] // 2
    got_b = swap(far[half:].astype(jnp.bfloat16), bits[-1])
    got_a = swap(far[:half].astype(jnp.bfloat16), bits[-1])
    got_n = swap((near[half:] + got_b).astype(jnp.bfloat16), bits[-2])
    total = near[:half] + got_a + got_n
    for bit in reversed(bits[:-2]):
        half = total.shape[0] // 2
        total = total[:half] + swap(total[half:].astype(jnp.bfloat16), bit)
    return total


def normalize(stream):
    mean_sq = jnp.mean(stream * stream, axis=-1, keepdims=True)
    scale_row = lax.rsqrt(mean_sq + 1e-06)
    return (stream * scale_row, scale_row)


def gelu_both(pre):
    root = math.sqrt(2.0 / math.pi)
    square = pre * pre
    tanh = jnp.tanh(root * pre * (1.0 + 0.044715 * square))
    gate = 0.5 + 0.5 * tanh
    slope = gate + 0.5 * pre * (1.0 - tanh * tanh) * root * (1.0 + 0.134145 * square)
    return (pre * gate).astype(jnp.bfloat16), slope


def dot(a, b):
    return jnp.dot(a, b, preferred_element_type=jnp.float32)


def shards(streams, cotangents, feed_streams, feed_cotangents, w_in, w_out, gain):
    first, second = streams[0, 0], streams[0, 1]
    grad_first, grad_second = cotangents[0, 0], cotangents[0, 1]
    weight_in, weight_out, gain_row = w_in[0], w_out[0], gain[0]
    hid = lax.axis_size("hid")
    bits = [1 << b for b in reversed(range(hid.bit_length() - 1))]
    at_top = lax.axis_index("section") == lax.axis_size("section") - 1
    tick_count = feed_streams.shape[0] + 1
    lifts, cots, hiddens, backs = [], [], [], []
    for tick_num in range(tick_count):
        last = tick_num == tick_count - 1
        normed, scale_row = normalize(first)
        lift = gather((normed * gain_row).astype(jnp.bfloat16), bits)
        cot = gather(grad_second.astype(jnp.bfloat16), bits)
        hidden, slope = zip(*[gelu_both(dot(rows, weight_in)) for rows in lift])
        block_out = reduce(*[dot(rows, weight_out) for rows in hidden], bits)
        back_pre = [
            (dot(rows, weight_out.T) * side).astype(jnp.bfloat16)
            for rows, side in zip(cot, slope)
        ]
        back_lift = reduce(*[dot(rows, weight_in.T) for rows in back_pre], bits)
        lifts += lift
        cots += cot
        hiddens += hidden
        backs += back_pre
        restored = second - block_out
        back_norm = back_lift * gain_row
        grad_stream = grad_first + scale_row * (
            back_norm - normed * jnp.mean(back_norm * normed, axis=-1, keepdims=True)
        )
        if last:
            new_streams = jnp.stack([restored, first])
            new_cot = jnp.stack([grad_second, grad_stream])
        else:
            kept = down(jnp.stack([first, grad_second]))
            feed, feed_cot = feed_streams[tick_num], feed_cotangents[tick_num]
            second = jnp.where(at_top, feed[1], kept[0])
            grad_first = jnp.where(at_top, feed_cot[0], kept[1])
            first = jnp.where(at_top, feed[0], down(restored))
            grad_second = jnp.where(at_top, feed_cot[1], down(grad_stream))
    total_in = dot(jnp.concatenate(lifts).T, jnp.concatenate(backs))
    total_out = dot(jnp.concatenate(hiddens).T, jnp.concatenate(cots))
    return (new_streams[None], new_cot[None], total_in[None], total_out[None])


def solution(mesh):
    placed = (
        P("section", None, "hid", None),
        P("section", None, "hid", None),
        P(None, None, "hid", None),
        P(None, None, "hid", None),
        P("section", None, "hid"),
        P("section", "hid", None),
        P("section", None),
    )
    return jax.shard_map(
        shards,
        mesh=mesh,
        in_specs=placed,
        out_specs=(
            P("section", None, "hid", None),
            P("section", None, "hid", None),
            P("section", None, "hid"),
            P("section", "hid", None),
        ),
        check_vma=False,
    )
```

```python
import math

import jax
import jax.numpy as jnp
from jax import lax
from jax.sharding import PartitionSpec as P


def swap(value, bit):
    count = lax.axis_size("hid")
    return lax.ppermute(value, "hid", [(i, i ^ bit) for i in range(count)])


def down(value):
    count = lax.axis_size("section")
    return lax.ppermute(value, "section", [(i, i - 1) for i in range(1, count)])


def gather(own, bits):
    near = own
    for bit in bits[:-2]:
        near = jnp.concatenate([near, swap(near, bit)], axis=0)
    near_b = swap(near, bits[-2])
    far_a = swap(near, bits[-1])
    far_b = swap(near_b, bits[-1])
    return (
        jnp.concatenate([near, near_b], axis=0),
        jnp.concatenate([far_a, far_b], axis=0),
    )


def reduce(near, far, bits):
    half = far.shape[0] // 2
    got_b = swap(far[half:].astype(jnp.bfloat16), bits[-1])
    got_a = swap(far[:half].astype(jnp.bfloat16), bits[-1])
    got_n = swap((near[half:] + got_b).astype(jnp.bfloat16), bits[-2])
    total = near[:half] + got_a + got_n
    for bit in reversed(bits[:-2]):
        half = total.shape[0] // 2
        total = total[:half] + swap(total[half:].astype(jnp.bfloat16), bit)
    return total


def normalize(stream):
    mean_sq = jnp.mean(stream * stream, axis=-1, keepdims=True)
    scale_row = lax.rsqrt(mean_sq + 1e-06)
    return (stream * scale_row, scale_row)


def gelu_both(pre):
    root = math.sqrt(2.0 / math.pi)
    square = pre * pre
    tanh = jnp.tanh(root * pre * (1.0 + 0.044715 * square))
    gate = 0.5 + 0.5 * tanh
    slope = gate + 0.5 * pre * (1.0 - tanh * tanh) * root * (1.0 + 0.134145 * square)
    return (pre * gate).astype(jnp.bfloat16), slope.astype(jnp.bfloat16)


def dot(a, b):
    return jnp.dot(a, b, preferred_element_type=jnp.float32)


def shards(streams, cotangents, feed_streams, feed_cotangents, w_in, w_out, gain):
    first, second = streams[0, 0], streams[0, 1]
    grad_first, grad_second = cotangents[0, 0], cotangents[0, 1]
    weight_in, weight_out, gain_row = w_in[0], w_out[0], gain[0]
    hid = lax.axis_size("hid")
    bits = [1 << b for b in reversed(range(hid.bit_length() - 1))]
    at_top = lax.axis_index("section") == lax.axis_size("section") - 1
    tick_count = feed_streams.shape[0] + 1
    lifts, cots, hiddens, backs = [], [], [], []
    for tick_num in range(tick_count):
        last = tick_num == tick_count - 1
        normed, scale_row = normalize(first)
        lift = gather((normed * gain_row).astype(jnp.bfloat16), bits)
        cot = gather(grad_second.astype(jnp.bfloat16), bits)
        hidden, slope = zip(*[gelu_both(dot(rows, weight_in)) for rows in lift])
        block_out = reduce(*[dot(rows, weight_out) for rows in hidden], bits)
        back_pre = [
            (dot(rows, weight_out.T) * side.astype(jnp.float32)).astype(jnp.bfloat16)
            for rows, side in zip(cot, slope)
        ]
        back_lift = reduce(*[dot(rows, weight_in.T) for rows in back_pre], bits)
        lifts += lift
        cots += cot
        hiddens += hidden
        backs += back_pre
        restored = second - block_out
        back_norm = back_lift * gain_row
        grad_stream = grad_first + scale_row * (
            back_norm - normed * jnp.mean(back_norm * normed, axis=-1, keepdims=True)
        )
        if last:
            new_streams = jnp.stack([restored, first])
            new_cot = jnp.stack([grad_second, grad_stream])
        else:
            kept = down(jnp.stack([first, grad_second]))
            feed, feed_cot = feed_streams[tick_num], feed_cotangents[tick_num]
            second = jnp.where(at_top, feed[1], kept[0])
            grad_first = jnp.where(at_top, feed_cot[0], kept[1])
            first = jnp.where(at_top, feed[0], down(restored))
            grad_second = jnp.where(at_top, feed_cot[1], down(grad_stream))
    total_in = dot(jnp.concatenate(lifts).T, jnp.concatenate(backs))
    total_out = dot(jnp.concatenate(hiddens).T, jnp.concatenate(cots))
    return (new_streams[None], new_cot[None], total_in[None], total_out[None])


def solution(mesh):
    placed = (
        P("section", None, "hid", None),
        P("section", None, "hid", None),
        P(None, None, "hid", None),
        P(None, None, "hid", None),
        P("section", None, "hid"),
        P("section", "hid", None),
        P("section", None),
    )
    return jax.shard_map(
        shards,
        mesh=mesh,
        in_specs=placed,
        out_specs=(
            P("section", None, "hid", None),
            P("section", None, "hid", None),
            P("section", None, "hid"),
            P("section", "hid", None),
        ),
        check_vma=False,
    )
```
